256 devices in a mesh: gx: 16 (over z, core), gy: 4 (over x), ens: 4 (over y).
Axes of the slice: x: 4, y: 4, z: 8, core: 2. Of those that a mesh axis runs over, the one named last changes fastest.
Arguments:
- state: float32 [16, 80, 128, 512], P(None, 'ens', 'gx', 'gy'), may hold values from -6 to 6
- obs_value: float32 [4, 256], replicated, may hold values from -6 to 6
- obs_error: float32 [4, 256], replicated, may hold values from 0.25 to 2
- obs_where: int32 [4, 3, 256], replicated, may hold values from 0 to 511, as said below
- radius: int32 [4, 256], replicated, may hold values from 33 to 43
- wind: float32 [2, 16, 128, 512], P(None, None, 'gx', 'gy'), may hold values from -0.4 to 0.4
Outputs:
- forecast: float32 [16, 80, 128, 512], P(None, 'ens', 'gx', 'gy')
The draws below stay inside these ranges and needn't reach their ends.
Inputs may be any that keep to these rules, and one draw needn't show every extreme that they name: obs_where[b, 0] is a level below 16, obs_where[b, 1] a row below 128, obs_where[b, 2] a column below 512.
All inputs are finite; a program needn't handle non-finite values.
Results may differ from the reference program's by a relative error of at most 0.00012.
Values sent between devices are 32-bit elements; how exact they have to be, the bound alone decides.
No kernel may reach another device: no remote copies, remote signals or barrier semaphores. Data moves between devices by JAX's collectives and lax.ppermute only.
A program may use at most 64 MiB of HBM per device.

```python
import math
import jax
import jax.numpy as jnp
from jax import lax

TILE_X = 8
LEVELS = 16
MEMBERS = 80
OBS = 256
BATCHES = 4
NX = 128
NY = 512


def draw_obs_where(key, part):
    keys = jax.random.split(jax.random.fold_in(key, 11), 8)
    shape = (BATCHES, OBS)
    levels = jax.random.randint(keys[0], shape, 0, LEVELS)
    flat_rows = jax.random.randint(keys[1], shape, 0, NX)
    flat_cols = jax.random.randint(keys[2], shape, 0, NY)
    hot_rows = jax.random.randint(keys[3], (BATCHES, 4), 0, NX)
    hot_cols = jax.random.randint(keys[4], (BATCHES, 4), 0, NY)
    picked = jax.random.randint(keys[5], shape, 0, 4)
    near_rows = jnp.take_along_axis(hot_rows, picked, axis=1) + jax.random.randint(keys[6], shape, -TILE_X, TILE_X + 1)
    near_cols = jnp.take_along_axis(hot_cols, picked, axis=1) + jax.random.randint(keys[7], shape, -TILE_X, TILE_X + 1)
    near_rows = jnp.clip(near_rows, 0, NX - 1)
    near_cols = jnp.clip(near_cols, 0, NY - 1)
    clustered = jnp.arange(OBS, dtype=jnp.int32)[None, :] >= OBS // 2
    rows = jnp.where(clustered, near_rows, flat_rows)
    cols = jnp.where(clustered, near_cols, flat_cols)
    levels = levels.at[0, 0].set(0).at[0, 1].set(LEVELS - 1)
    rows = rows.at[0, 0].set(0).at[0, 1].set(NX - 1)
    cols = cols.at[0, 0].set(0).at[0, 1].set(NY - 1)
    return jnp.stack([levels, rows, cols], axis=1).astype(jnp.int32)


def place_ends(values, own_key, low, largest):
    place = [jax.random.randint(jax.random.fold_in(own_key, axis), (), 0, length) for axis, length in enumerate(values.shape)]
    main_axis = values.shape.index(max(values.shape))
    beside = place[:main_axis] + [(place[main_axis] + 1) % values.shape[main_axis]] + place[main_axis + 1:]
    return values.at[tuple(place)].set(low).at[tuple(beside)].set(largest)


def block_levels(stream_key, shape, cuts, smallest, largest):
    level = 1.0
    for axis_at, blocks in cuts:
        heights = jax.random.uniform(jax.random.fold_in(jax.random.fold_in(stream_key, 6), axis_at), (blocks,), jnp.float32, smallest / len(cuts), largest / len(cuts))
        level = level * jnp.repeat(jnp.exp(heights), shape[axis_at] // blocks).reshape((-1,) + (1,) * (len(shape) - 1 - axis_at))
    return level


def noise(own_key, extent, scale, bound, pieces=(), held_as=jnp.bfloat16):
    array = scale * jax.random.normal(own_key, extent, jnp.float32)
    if pieces:
        array = array * block_levels(own_key, extent, pieces, -0.22, 0.18)
    return jnp.clip(array, -bound, bound).astype(held_as)


def setup_inputs(seed: int = 0) -> dict:
    streams_of = jax.random.split(jax.random.key(seed), 7)
    state = noise(streams_of[0], (LEVELS, MEMBERS, NX, NY), 1.0, 6.0, ((1, 4), (2, 16), (3, 4)), jnp.float32)
    obs_value = noise(streams_of[1], (BATCHES, OBS), 1.0, 6.0, (), jnp.float32)
    obs_error = jnp.clip(jnp.exp(jax.random.uniform(streams_of[2], (BATCHES, OBS), jnp.float32, math.log(0.25), math.log(2.0))), 0.25, 2.0)
    obs_where = draw_obs_where(jax.random.fold_in(streams_of[6], 71), 0)
    radius = place_ends(jax.random.randint(streams_of[4], (BATCHES, OBS), NX // 4 + 1, NX // 3 + 2), jax.random.fold_in(streams_of[4], 1), NX // 4 + 1, (NX // 3 + 2) - 1).astype(jnp.int32)
    wind = jnp.clip(jax.random.uniform(streams_of[5], (2, LEVELS, NX, NY), jnp.float32, -0.4, 0.4) * block_levels(streams_of[5], (2, LEVELS, NX, NY), ((2, 16), (3, 4)), -0.4, 0.0), -0.4, 0.4)
    return dict(state=state, obs_value=obs_value, obs_error=obs_error, obs_where=obs_where, radius=radius, wind=wind)


EPSILON = 1e-06
DIFFUSE = 0.05

def increments(priors, value, error):
    members = priors.shape[1]
    center = lax.optimization_barrier(jnp.mean(priors, axis=1))
    spread = priors - center[:, None]
    variance = lax.optimization_barrier(jnp.sum(spread * spread, axis=1)) / (members - 1)
    summed = variance + error
    post_mean = (error * center + variance * value) / summed
    factor = jnp.sqrt(error / summed)
    nudges = post_mean[:, None] + factor[:, None] * spread - priors
    inverse = 1.0 / ((members - 1) * (variance + EPSILON))
    return (spread, nudges, inverse)

def tapering(dist_sq, radii):
    reach_sq = (4 * radii * radii).astype(jnp.float32)
    weight = jnp.maximum(0.0, 1.0 - dist_sq.astype(jnp.float32) / reach_sq)
    return weight * weight

def stencil(values, padded, wind):
    above = padded[:, :, :-2, 1:-1]
    below = padded[:, :, 2:, 1:-1]
    left_cell = padded[:, :, 1:-1, :-2]
    right_cell = padded[:, :, 1:-1, 2:]
    wind_rows = wind[0][:, None]
    wind_cols = wind[1][:, None]
    flux = jnp.maximum(wind_rows, 0.0) * (values - above) + jnp.minimum(wind_rows, 0.0) * (below - values)
    flux = flux + jnp.maximum(wind_cols, 0.0) * (values - left_cell) + jnp.minimum(wind_cols, 0.0) * (right_cell - values)
    return values - flux + DIFFUSE * (above + below + left_cell + right_cell - 4.0 * values)

def assimilate(current, value, error, places, radii):
    priors = current[places[0], :, places[1], places[2]]
    spread, nudges, inverse = increments(priors, value, error)
    anomaly = current - lax.optimization_barrier(jnp.mean(current, axis=1, keepdims=True))
    grid_rows = jnp.arange(NX, dtype=jnp.int32)
    grid_cols = jnp.arange(NY, dtype=jnp.int32)
    diff_rows = grid_rows[None, :] - places[1][:, None]
    diff_cols = grid_cols[None, :] - places[2][:, None]
    dist_sq = (diff_rows[:, :, None] * diff_rows[:, :, None] + diff_cols[:, None, :] * diff_cols[:, None, :]).reshape(OBS, NX * NY)
    weight = tapering(dist_sq, radii[:, None])

    def level_change(level_anomaly):
        flat = level_anomaly.reshape(MEMBERS, NX * NY)
        covar = jnp.dot(spread, flat, precision=lax.Precision.HIGHEST)
        gain_map = weight * covar * inverse[:, None]
        return jnp.dot(nudges.T, gain_map, precision=lax.Precision.HIGHEST).reshape(MEMBERS, NX, NY)
    change = lax.map(level_change, anomaly)
    return current + change

def reference(state, obs_value, obs_error, obs_where, radius, wind):
    current = state
    for batch in range(BATCHES):
        current = assimilate(current, obs_value[batch], obs_error[batch], obs_where[batch], radius[batch])
    padded = jnp.pad(current, ((0, 0), (0, 0), (1, 1), (1, 1)))
    return stencil(current, padded, wind)
```

```python
import jax
import jax.numpy as jnp
from jax import lax
from jax.experimental import pallas as pl
from jax.experimental.pallas import tpu as pltpu
from jax.sharding import Mesh
from jax.sharding import PartitionSpec as P

GX = ("gx_0", "gx_1")
EPSILON = 1e-06
DIFFUSE = 0.05
F32 = jnp.float32
BF16 = jnp.bfloat16
VMEM = pltpu.VMEM
SMEM = pltpu.SMEM


def split(x):
    high = x.astype(BF16)
    return high, (x - high.astype(F32)).astype(BF16)


def pick_kernel(place_ref, where_ref, state_ref, keep_ref, give_ref, parts_ref, found_ref):
    row_start, col_start, core = place_ref[0], place_ref[1], place_ref[2]
    cells = state_ref.shape[0] // 8
    levels = found_ref.shape[0] // keep_ref.shape[0]
    members = keep_ref.shape[0]
    cols = state_ref.shape[1]
    n_obs = where_ref.shape[2]
    halves = where_ref.shape[0] // 2
    for row in range(8):
        x = state_ref[pl.ds(row, cells, stride=8), :]
        high = x.astype(BF16)
        rest = x - high.astype(F32)
        mid = rest.astype(BF16)
        low = (rest - mid.astype(F32)).astype(BF16)
        for at, part in enumerate((high, mid, low)):
            parts_ref[at * cells : (at + 1) * cells, row * cols : (row + 1) * cols] = part
    cell = lax.broadcasted_iota(jnp.int32, (8 * cols, n_obs), 0)
    for half, out_ref in enumerate((keep_ref, give_ref)):
        for at in range(halves):
            batch = lax.rem(core + half, 2) * halves + at
            places = where_ref[batch]
            lev = places[0:1, :]
            row = places[1:2, :] - row_start
            col = places[2:3, :] - col_start
            owned = (row >= 0) & (row < 8) & (col >= 0) & (col < cols)
            key = jnp.where(owned, row * cols + col, -1)
            hot = jnp.where(cell == key, 1.0, 0.0).astype(BF16)
            got = jnp.dot(parts_ref[...], hot, preferred_element_type=F32)
            found_ref[...] = got[:cells] + got[cells : 2 * cells] + got[2 * cells :]
            total = jnp.zeros((members, n_obs), F32)
            for level in range(levels):
                rows = found_ref[level * members : (level + 1) * members, :]
                total = total + jnp.where(lev == level, rows, 0.0)
            out_ref[:, at * n_obs : (at + 1) * n_obs] = total


def taper(dist_sq, reach):
    weight = jnp.maximum(0.0, 1.0 - dist_sq * reach)
    return weight * weight


def down(row):
    return jnp.transpose(jnp.broadcast_to(row, (128, row.shape[1])))


def wide(block, lanes):
    return jnp.concatenate([block] * (lanes // 128), axis=1)


def lay_kernel(place_ref, where_ref, radius_ref, cur_ref, y_ref, top_ref, low_ref, left_ref, right_ref, w_ref, wc_ref, wo_ref):
    row_start, col_start, me = place_ref[0], place_ref[1], place_ref[3]
    batches, _, n_obs = where_ref.shape
    cols = cur_ref.shape[1]
    shares = 4
    levels = y_ref.shape[2] // cols
    members = y_ref.shape[1] // shares
    for share in range(shares):
        source = lax.rem(me + share, shares)
        for level in range(levels):
            base = (source * levels + level) * members * 8
            for row in range(8):
                got = cur_ref[pl.ds(base + row, members, stride=8), :]
                y_ref[row, share * members : (share + 1) * members, level * cols : (level + 1) * cols] = got
    top_ref[...] = y_ref[0]
    low_ref[...] = y_ref[7]
    lane = lax.broadcasted_iota(jnp.int32, left_ref.shape, 1)
    left = jnp.zeros(left_ref.shape, F32)
    right = jnp.zeros(left_ref.shape, F32)
    for level in range(levels):
        for row in range(8):
            x = y_ref[row, :, level * cols : (level + 1) * cols]
            at = level * 8 + row
            left = jnp.where(lane == 32 + at, pltpu.roll(x, 32 + at, 1), left)
            right = jnp.where(lane == at, pltpu.roll(x, (at + 1) % cols, 1), right)
    left_ref[...] = left
    right_ref[...] = right
    lane_w = lax.broadcasted_iota(jnp.int32, (n_obs, cols), 1)
    for batch in range(batches):
        places = where_ref[batch].astype(F32)
        q = radius_ref[batch : batch + 1, :].astype(F32)
        obs_row, obs_col = down(places[1:2, :]), down(places[2:3, :])
        reach = down(1.0 / (4.0 * q * q))
        gap = (lane_w + col_start).astype(F32) - obs_col
        gap = gap * gap
        for row in range(10):
            off = (row_start + (row - 1)).astype(F32) - obs_row
            w_ref[batch * 10 + row] = taper(off * off + gap, reach)
        edge_row = (row_start + lane_w % 8).astype(F32) - obs_row
        edge_col = jnp.where(lane_w < 32, col_start - 1, col_start + cols).astype(F32) - obs_col
        wc_ref[batch] = taper(edge_row * edge_row + edge_col * edge_col, reach)
        for later in range(batch + 1, batches):
            others = where_ref[later].astype(F32)
            off = others[1:2, :] - wide(obs_row, n_obs)
            gap_o = others[2:3, :] - wide(obs_col, n_obs)
            pair = batch * (2 * batches - batch - 1) // 2 + later - batch - 1
            wo_ref[pair] = taper(off * off + gap_o * gap_o, wide(reach, n_obs))


def changed(x, weights, s3_ref, n2_ref):
    members = x.shape[0]
    mean = jnp.sum(x, axis=0, keepdims=True) * (1.0 / members)
    a_high, a_low = split(x - mean)
    covar = jnp.dot(s3_ref[...], jnp.concatenate([a_high, a_high, a_low], axis=0), preferred_element_type=F32)
    g_high, g_low = split(weights * covar)
    both = jnp.dot(n2_ref[...], g_high, preferred_element_type=F32)
    return x + ((both[:members] + both[members:]) + jnp.dot(n2_ref[:members, :], g_low, preferred_element_type=F32))


def main_kernel(
    place_ref, value_ref, error_ref, own_ref, one_ref, two_ref, three_ref, other_ref,
    y_ref, up_ref, down_ref, left_ref, right_ref, w_ref, wc_ref, wo_ref, wind_ref,
    out_ref, prior_ref, z_ref, edge_ref, s3_ref, n2_ref, f_ref,
):
    core, me, lev_start = place_ref[2], place_ref[3], place_ref[4]
    batches, n_obs = value_ref.shape
    members = z_ref.shape[1]
    shares = 4
    share_size = members // shares
    cols = w_ref.shape[2]
    levels = z_ref.shape[2] // cols
    half = own_ref.shape[1]
    for share, ref in enumerate((own_ref, one_ref, two_ref, three_ref)):
        rows = slice(share * share_size, (share + 1) * share_size)
        prior_ref[core, rows, :] = ref[...]
        prior_ref[1 - core, rows, :] = other_ref[share]
    z_ref[0] = up_ref[...]
    z_ref[9] = down_ref[...]
    for row in range(8):
        z_ref[row + 1] = y_ref[row]
    edge_ref[...] = left_ref[...] + right_ref[...]
    per_half = half // n_obs

    def lanes(batch):
        at = batch % per_half
        return batch // per_half, slice(at * n_obs, (at + 1) * n_obs)

    for batch in range(batches):
        part, here = lanes(batch)
        priors = prior_ref[part, :, here]
        value, error = value_ref[batch : batch + 1, :], error_ref[batch : batch + 1, :]
        center = jnp.sum(priors, axis=0, keepdims=True) * (1.0 / members)
        spread = priors - center
        variance = jnp.sum(spread * spread, axis=0, keepdims=True) / (members - 1)
        summed = variance + error
        post_mean = (error * center + variance * value) / summed
        factor = jnp.sqrt(error / summed)
        nudges = post_mean + factor * spread - priors
        inverse = 1.0 / ((members - 1) * (variance + EPSILON))
        n_high, n_low = split(nudges * inverse)
        n2_ref[...] = jnp.concatenate([n_high, n_low], axis=0)
        s_high, s_low = split(spread)
        s3 = jnp.concatenate([s_high.astype(F32), s_low.astype(F32), s_high.astype(F32)], axis=0)
        s3_ref[...] = jnp.transpose(s3).astype(BF16)
        for later in range(batch + 1, batches):
            pair = batch * (2 * batches - batch - 1) // 2 + later - batch - 1
            part, there = lanes(later)
            prior_ref[part, :, there] = changed(prior_ref[part, :, there], wo_ref[pair], s3_ref, n2_ref)

        def step(at, carry):
            for row in (2 * at, 2 * at + 1):
                weights = wide(w_ref[batch * 10 + row], levels * cols)
                z_ref[row] = changed(z_ref[row], weights, s3_ref, n2_ref)
            return carry

        lax.fori_loop(0, 5, step, 0)
        edge_ref[...] = changed(edge_ref[...], wc_ref[batch], s3_ref, n2_ref)

    lane = lax.broadcasted_iota(jnp.int32, (members, cols), 1)

    def transport(row, carry):
        edge = edge_ref[...]
        for level in range(levels):
            span = slice(level * cols, (level + 1) * cols)
            a = wind_ref[0, lev_start + level, pl.ds(row, 1), :]
            b = wind_ref[1, lev_start + level, pl.ds(row, 1), :]
            to_up = jnp.maximum(a, 0.0) + DIFFUSE
            to_down = DIFFUSE - jnp.minimum(a, 0.0)
            to_left = jnp.maximum(b, 0.0) + DIFFUSE
            to_right = DIFFUSE - jnp.minimum(b, 0.0)
            stay = 1.0 - ((to_up + to_down) + (to_left + to_right))
            x = z_ref[row + 1, :, span]
            at = level * 8 + row
            left = jnp.where(lane == 0, pltpu.roll(edge, lax.rem(cols - at, cols), 1), pltpu.roll(x, 1, 1))
            right = jnp.where(
                lane == cols - 1, pltpu.roll(edge, cols - 33 - at, 1), pltpu.roll(x, cols - 1, 1)
            )
            f_ref[...] = (
                stay * x + to_up * z_ref[row, :, span] + to_down * z_ref[row + 2, :, span]
                + to_left * left + to_right * right
            )
            for share in range(shares):
                target = lax.rem(me + share, shares)
                base = (target * levels + level) * share_size * 8
                out_ref[pl.ds(base + row, share_size, stride=8), :] = f_ref[
                    share * share_size : (share + 1) * share_size, :
                ]
        return carry

    lax.fori_loop(0, 8, transport, 0)


def ring(axis, shift):
    n = lax.axis_size(axis)
    return [(i, (i + shift) % n) for i in range(n)]


def line(axis, shift):
    n = lax.axis_size(axis)
    return [(i, i + shift) for i in range(n) if 0 <= i + shift < n]


def total_of(keep, give):
    x = keep + lax.ppermute(give, "gx_1", ring("gx_1", 1))
    x = x + lax.ppermute(x, "gy", [(i, i ^ 1) for i in range(4)])
    x = x + lax.ppermute(x, "gy", [(i, i ^ 2) for i in range(4)])
    low, high = lax.ppermute(x, "gx_0", ring("gx_0", 1)), lax.ppermute(x, "gx_0", ring("gx_0", -1))
    two = x + low
    three = two + high
    return three + lax.ppermute(three, "gx_0", ring("gx_0", 3)) + lax.ppermute(two, "gx_0", ring("gx_0", -3))


def shards(state, obs_value, obs_error, obs_where, radius, wind):
    levels, share_size, tile_rows, tile_cols = state.shape
    shares = lax.axis_size("ens")
    members = share_size * shares
    here = levels // shares
    batches, n_obs = obs_value.shape
    half = batches // 2 * n_obs
    me = lax.axis_index("ens")
    place = jnp.stack(
        [lax.axis_index(GX) * tile_rows, lax.axis_index("gy") * tile_cols, lax.axis_index("gx_1"), me, me * here]
    ).astype(jnp.int32)
    flat = levels * share_size * tile_rows
    cur = lax.all_to_all(state, "ens", split_axis=0, concat_axis=0, tiled=True)
    vmem = pl.BlockSpec(memory_space=VMEM)
    smem = pl.BlockSpec(memory_space=SMEM)
    cells = levels * share_size
    keep, give = pl.pallas_call(
        pick_kernel,
        out_shape=[jax.ShapeDtypeStruct((share_size, half), F32)] * 2,
        in_specs=[smem, vmem, vmem],
        out_specs=[vmem, vmem],
        scratch_shapes=[VMEM((3 * cells, tile_rows * tile_cols), BF16), VMEM((cells, n_obs), F32)],
        compiler_params=pltpu.CompilerParams(vmem_limit_bytes=16 << 20),
        name="pick",
    )(place, obs_where, state.reshape(flat, tile_cols))
    own = total_of(keep, give)
    one, two, three = (lax.ppermute(own, "ens", ring("ens", -k)) for k in (1, 2, 3))
    other = lax.ppermute(jnp.stack([own, one, two, three]), "gx_1", ring("gx_1", 1))
    pairs = batches * (batches - 1) // 2
    line_shape = jax.ShapeDtypeStruct((members, here * tile_cols), F32)
    edge_shape = jax.ShapeDtypeStruct((members, tile_cols), F32)
    y, top, low, left, right, w, wc, wo = pl.pallas_call(
        lay_kernel,
        out_shape=[
            jax.ShapeDtypeStruct((tile_rows, members, here * tile_cols), F32),
            line_shape, line_shape, edge_shape, edge_shape,
            jax.ShapeDtypeStruct((batches * 10, n_obs, tile_cols), F32),
            jax.ShapeDtypeStruct((batches, n_obs, tile_cols), F32),
            jax.ShapeDtypeStruct((pairs, n_obs, n_obs), F32),
        ],
        in_specs=[smem, vmem, vmem, vmem],
        out_specs=[vmem] * 8,
        compiler_params=pltpu.CompilerParams(vmem_limit_bytes=24 << 20),
        name="lay",
    )(place, obs_where, radius, cur.reshape(flat, tile_cols))
    up = lax.ppermute(low, GX, line(GX, 1))
    down_ = lax.ppermute(top, GX, line(GX, -1))
    from_left = lax.ppermute(right, "gy", line("gy", 1))
    from_right = lax.ppermute(left, "gy", line("gy", -1))
    out = pl.pallas_call(
        main_kernel,
        out_shape=jax.ShapeDtypeStruct((flat, tile_cols), F32),
        in_specs=[smem] + [vmem] * 16,
        out_specs=vmem,
        scratch_shapes=[
            VMEM((2, members, half), F32),
            VMEM((tile_rows + 2, members, here * tile_cols), F32),
            VMEM((members, tile_cols), F32),
            VMEM((n_obs, 3 * members), BF16),
            VMEM((2 * members, n_obs), BF16),
            VMEM((members, tile_cols), F32),
        ],
        compiler_params=pltpu.CompilerParams(vmem_limit_bytes=32 << 20),
        name="main",
    )(
        place, obs_value, obs_error, own, one, two, three, other,
        y, up, down_, from_left, from_right, w, wc, wo, wind,
    )
    out = out.reshape(levels, share_size, tile_rows, tile_cols)
    return lax.all_to_all(out, "ens", split_axis=0, concat_axis=0, tiled=True)


def solution(mesh):
    torus = Mesh(
        mesh.devices.reshape(8, 2, mesh.shape["gy"], mesh.shape["ens"]),
        ("gx_0", "gx_1", "gy", "ens"),
    )
    placed = (P(None, "ens", GX, "gy"), P(), P(), P(), P(), P(None, None, GX, "gy"))
    return jax.shard_map(
        shards, mesh=torus, in_specs=placed, out_specs=P(None, "ens", GX, "gy"), check_vma=False
    )
```

```python
import jax
import jax.numpy as jnp
from jax import lax
from jax.experimental import pallas as pl
from jax.experimental.pallas import tpu as pltpu
from jax.sharding import Mesh
from jax.sharding import PartitionSpec as P


GX = ("gx_0", "gx_1")
EPSILON = 1e-06
DIFFUSE = 0.05
F32 = jnp.float32
BF16 = jnp.bfloat16
ROWS = 2
VMEM = pltpu.VMEM
SMEM = pltpu.SMEM


def split(x):
    high = x.astype(BF16)
    return high, (x - high.astype(F32)).astype(BF16)


def pick_kernel(place_ref, where_ref, state_ref, keep_ref, give_ref, parts_ref, found_ref):
    row_start, col_start, core = place_ref[0], place_ref[1], place_ref[2]
    cells = state_ref.shape[0] // 8
    levels = found_ref.shape[0] // keep_ref.shape[0]
    members = keep_ref.shape[0]
    cols = state_ref.shape[1]
    n_obs = where_ref.shape[2]
    halves = where_ref.shape[0] // 2
    for row in range(8):
        x = state_ref[pl.ds(row, cells, stride=8), :]
        high = x.astype(BF16)
        rest = x - high.astype(F32)
        mid = rest.astype(BF16)
        low = (rest - mid.astype(F32)).astype(BF16)
        for at, part in enumerate((high, mid, low)):
            parts_ref[at * cells : (at + 1) * cells, row * cols : (row + 1) * cols] = part
    cell = lax.broadcasted_iota(jnp.int32, (8 * cols, n_obs), 0)
    for half, out_ref in enumerate((keep_ref, give_ref)):
        for at in range(halves):
            batch = lax.rem(core + half, 2) * halves + at
            places = where_ref[batch]
            lev = places[0:1, :]
            row = places[1:2, :] - row_start
            col = places[2:3, :] - col_start
            owned = (row >= 0) & (row < 8) & (col >= 0) & (col < cols)
            key = jnp.where(owned, row * cols + col, -1)
            hot = jnp.where(cell == key, 1.0, 0.0).astype(BF16)
            got = jnp.dot(parts_ref[...], hot, preferred_element_type=F32)
            found_ref[...] = got[:cells] + got[cells : 2 * cells] + got[2 * cells :]
            total = jnp.zeros((members, n_obs), F32)
            for level in range(levels):
                rows = found_ref[level * members : (level + 1) * members, :]
                total = total + jnp.where(lev == level, rows, 0.0)
            out_ref[:, at * n_obs : (at + 1) * n_obs] = total


def taper(dist_sq, reach):
    weight = jnp.maximum(0.0, 1.0 - dist_sq * reach)
    return weight * weight


def down(row):
    return jnp.transpose(jnp.broadcast_to(row, (128, row.shape[1])))


def wide(block, lanes):
    return jnp.concatenate([block] * (lanes // 128), axis=1)


def lay_kernel(place_ref, cur_ref, after_ref, y_ref, top_ref, low_ref, left_ref, right_ref):
    me = place_ref[3]
    cols = cur_ref.shape[1]
    shares = 4
    levels = y_ref.shape[2] // cols
    members = y_ref.shape[1] // shares
    for share in range(shares):
        source = lax.rem(me + share, shares)
        for level in range(levels):
            base = (source * levels + level) * members * 8
            for row in range(8):
                got = cur_ref[pl.ds(base + row, members, stride=8), :]
                y_ref[row, share * members : (share + 1) * members, level * cols : (level + 1) * cols] = got
    top_ref[...] = y_ref[0]
    low_ref[...] = y_ref[7]
    lane = lax.broadcasted_iota(jnp.int32, left_ref.shape, 1)
    left = jnp.zeros(left_ref.shape, F32)
    right = jnp.zeros(left_ref.shape, F32)
    for level in range(levels):
        for row in range(8):
            x = y_ref[row, :, level * cols : (level + 1) * cols]
            at = level * 8 + row
            left = jnp.where(lane == 32 + at, pltpu.roll(x, 32 + at, 1), left)
            right = jnp.where(lane == at, pltpu.roll(x, (at + 1) % cols, 1), right)
    left_ref[...] = left
    right_ref[...] = right


def taper_kernel(place_ref, where_ref, radius_ref, after_ref, w_ref, wc_ref, wo_ref):
    row_start, col_start = place_ref[0], place_ref[1]
    batches, _, n_obs = where_ref.shape
    cols = w_ref.shape[2]
    lane_w = lax.broadcasted_iota(jnp.int32, (n_obs, cols), 1)
    for batch in range(batches):
        places = where_ref[batch].astype(F32)
        q = radius_ref[batch : batch + 1, :].astype(F32)
        obs_row, obs_col = down(places[1:2, :]), down(places[2:3, :])
        reach = down(1.0 / (4.0 * q * q))
        gap = (lane_w + col_start).astype(F32) - obs_col
        gap = gap * gap
        for row in range(10):
            off = (row_start + (row - 1)).astype(F32) - obs_row
            w_ref[batch * 10 + row] = taper(off * off + gap, reach)
        edge_row = (row_start + lane_w % 8).astype(F32) - obs_row
        edge_col = jnp.where(lane_w < 32, col_start - 1, col_start + cols).astype(F32) - obs_col
        wc_ref[batch] = taper(edge_row * edge_row + edge_col * edge_col, reach)
        for later in range(batch + 1, batches):
            others = where_ref[later].astype(F32)
            off = others[1:2, :] - wide(obs_row, n_obs)
            gap_o = others[2:3, :] - wide(obs_col, n_obs)
            pair = batch * (2 * batches - batch - 1) // 2 + later - batch - 1
            wo_ref[pair] = taper(off * off + gap_o * gap_o, wide(reach, n_obs))


def changed(xs, weights, s3, n2):
    members = xs[0].shape[0]
    stacks = []
    for x in xs:
        mean = jnp.sum(x, axis=0, keepdims=True) * (1.0 / members)
        a_high, a_low = split(x - mean)
        stacks.append(jnp.concatenate([a_high, a_high, a_low], axis=0))
    covars = [jnp.dot(s3, a3, preferred_element_type=F32) for a3 in stacks]
    gains = [split(w * c) for w, c in zip(weights, covars)]
    outs = []
    for x, (g_high, g_low) in zip(xs, gains):
        both = jnp.dot(n2, g_high, preferred_element_type=F32)
        rest = jnp.dot(n2[:members], g_low, preferred_element_type=F32)
        outs.append(x + ((both[:members] + both[members:]) + rest))
    return outs


def main_kernel(
    place_ref, value_ref, error_ref, own_ref, one_ref, two_ref, three_ref, other_ref,
    y_ref, up_ref, down_ref, left_ref, right_ref, w_ref, wc_ref, wo_ref, wind_ref,
    out_ref, prior_ref, z_ref, edge_ref, s3_ref, n2_ref, f_ref,
):
    core, me, lev_start = place_ref[2], place_ref[3], place_ref[4]
    batches, n_obs = value_ref.shape
    members = z_ref.shape[1]
    shares = 4
    share_size = members // shares
    cols = w_ref.shape[2]
    levels = z_ref.shape[2] // cols
    half = own_ref.shape[1]
    for share, ref in enumerate((own_ref, one_ref, two_ref, three_ref)):
        rows = slice(share * share_size, (share + 1) * share_size)
        prior_ref[core, rows, :] = ref[...]
        prior_ref[1 - core, rows, :] = other_ref[share]
    z_ref[0] = up_ref[...]
    z_ref[9] = down_ref[...]
    for row in range(8):
        z_ref[row + 1] = y_ref[row]
    edge_ref[...] = left_ref[...] + right_ref[...]
    per_half = half // n_obs

    def lanes(batch):
        at = batch % per_half
        return batch // per_half, slice(at * n_obs, (at + 1) * n_obs)

    for batch in range(batches):
        part, here = lanes(batch)
        priors = prior_ref[part, :, here]
        value, error = value_ref[batch : batch + 1, :], error_ref[batch : batch + 1, :]
        center = jnp.sum(priors, axis=0, keepdims=True) * (1.0 / members)
        spread = priors - center
        variance = jnp.sum(spread * spread, axis=0, keepdims=True) / (members - 1)
        summed = variance + error
        post_mean = (error * center + variance * value) / summed
        factor = jnp.sqrt(error / summed)
        nudges = post_mean + factor * spread - priors
        inverse = 1.0 / ((members - 1) * (variance + EPSILON))
        n_high, n_low = split(nudges * inverse)
        n2_ref[...] = jnp.concatenate([n_high, n_low], axis=0)
        s_high, s_low = split(spread)
        s3 = jnp.concatenate([s_high.astype(F32), s_low.astype(F32), s_high.astype(F32)], axis=0)
        s3_ref[...] = jnp.transpose(s3).astype(BF16)
        laters = range(batch + 1, batches)
        first = batch * (2 * batches - batch - 1) // 2
        blocks = [edge_ref[...]] + [prior_ref[lanes(k)[0], :, lanes(k)[1]] for k in laters]
        tapers = [wc_ref[batch]] + [wo_ref[first + k] for k in range(len(laters))]
        blocks = changed(blocks, tapers, s3_ref[...], n2_ref[...])
        edge_ref[...] = blocks[0]
        for k, block in zip(laters, blocks[1:]):
            prior_ref[lanes(k)[0], :, lanes(k)[1]] = block

        def step(at, carry):
            rows = [ROWS * at + k for k in range(ROWS)]
            xs = [z_ref[row, :, k * 256 : (k + 1) * 256] for row in rows for k in range(2)]
            ws = [wide(w_ref[batch * 10 + row], 256) for row in rows for _ in range(2)]
            outs = changed(xs, ws, s3_ref[...], n2_ref[...])
            for at_out, out in enumerate(outs):
                k = at_out % 2
                z_ref[rows[at_out // 2], :, k * 256 : (k + 1) * 256] = out
            return carry

        lax.fori_loop(0, 10 // ROWS, step, 0)

    lane = lax.broadcasted_iota(jnp.int32, (members, cols), 1)

    def transport(row, carry):
        edge = edge_ref[...]
        for level in range(levels):
            span = slice(level * cols, (level + 1) * cols)
            a = wind_ref[0, lev_start + level, pl.ds(row, 1), :]
            b = wind_ref[1, lev_start + level, pl.ds(row, 1), :]
            to_up = jnp.maximum(a, 0.0) + DIFFUSE
            to_down = DIFFUSE - jnp.minimum(a, 0.0)
            to_left = jnp.maximum(b, 0.0) + DIFFUSE
            to_right = DIFFUSE - jnp.minimum(b, 0.0)
            stay = 1.0 - ((to_up + to_down) + (to_left + to_right))
            x = z_ref[row + 1, :, span]
            at = level * 8 + row
            left = jnp.where(lane == 0, pltpu.roll(edge, lax.rem(cols - at, cols), 1), pltpu.roll(x, 1, 1))
            right = jnp.where(
                lane == cols - 1, pltpu.roll(edge, cols - 33 - at, 1), pltpu.roll(x, cols - 1, 1)
            )
            f_ref[...] = (
                stay * x + to_up * z_ref[row, :, span] + to_down * z_ref[row + 2, :, span]
                + to_left * left + to_right * right
            )
            for share in range(shares):
                target = lax.rem(me + share, shares)
                base = (target * levels + level) * share_size * 8
                out_ref[pl.ds(base + row, share_size, stride=8), :] = f_ref[
                    share * share_size : (share + 1) * share_size, :
                ]
        return carry

    lax.fori_loop(0, 8, transport, 0)


def ring(axis, shift):
    n = lax.axis_size(axis)
    return [(i, (i + shift) % n) for i in range(n)]


def line(axis, shift):
    n = lax.axis_size(axis)
    return [(i, i + shift) for i in range(n) if 0 <= i + shift < n]


def exchanges():
    cores = lax.axis_size("gx_1")
    depth, across = lax.axis_size("gx_0"), lax.axis_size("gy")
    far = [1 << k for k in range(depth.bit_length() - 1)]
    near = [1 << k for k in range(across.bit_length() - 1)]
    orders = (
        [("x", b) for b in near] + [("z", b) for b in far],
        [("z", b) for b in reversed(far)] + [("x", b) for b in near],
    )
    steps = []
    for at in range(len(orders[0])):
        pairs = []
        for z in range(depth):
            for core in range(cores):
                for x in range(across):
                    axis, bit = orders[core % 2][at]
                    to_z, to_x = (z ^ bit, x) if axis == "z" else (z, x ^ bit)
                    pairs.append(((z * cores + core) * across + x, (to_z * cores + core) * across + to_x))
        steps.append(pairs)
    return steps


def shards(state, obs_value, obs_error, obs_where, radius, wind):
    levels, share_size, tile_rows, tile_cols = state.shape
    shares = lax.axis_size("ens")
    members = share_size * shares
    here = levels // shares
    batches, n_obs = obs_value.shape
    half = batches // 2 * n_obs
    me = lax.axis_index("ens")
    place = jnp.stack(
        [lax.axis_index(GX) * tile_rows, lax.axis_index("gy") * tile_cols, lax.axis_index("gx_1"), me, me * here]
    ).astype(jnp.int32)
    flat = levels * share_size * tile_rows
    vmem = pl.BlockSpec(memory_space=VMEM)
    smem = pl.BlockSpec(memory_space=SMEM)
    cells = levels * share_size
    keep, give = pl.pallas_call(
        pick_kernel,
        out_shape=[jax.ShapeDtypeStruct((share_size, half), F32)] * 2,
        in_specs=[smem, vmem, vmem],
        out_specs=[vmem, vmem],
        scratch_shapes=[VMEM((3 * cells, tile_rows * tile_cols), BF16), VMEM((cells, n_obs), F32)],
        compiler_params=pltpu.CompilerParams(vmem_limit_bytes=16 << 20),
        name="pick",
    )(place, obs_where, state.reshape(flat, tile_cols))
    any_ = pl.BlockSpec(memory_space=pl.ANY)
    cur = lax.all_to_all(state, "ens", split_axis=0, concat_axis=0, tiled=True)
    x = keep + lax.ppermute(give, "gx_1", ring("gx_1", 1))
    for step, pairs in enumerate(exchanges(), start=1):
        got = lax.ppermute(x, (*GX, "gy"), pairs)
        if step == 3:
            line_shape = jax.ShapeDtypeStruct((members, here * tile_cols), F32)
            edge_shape = jax.ShapeDtypeStruct((members, tile_cols), F32)
            y, top, low, left, right = pl.pallas_call(
                lay_kernel,
                out_shape=[
                    jax.ShapeDtypeStruct((tile_rows, members, here * tile_cols), F32),
                    line_shape, line_shape, edge_shape, edge_shape,
                ],
                in_specs=[smem, vmem, any_],
                out_specs=[vmem] * 5,
                compiler_params=pltpu.CompilerParams(vmem_limit_bytes=12 << 20),
                cost_estimate=pl.CostEstimate(flops=2_000_000, bytes_accessed=4_000_000, transcendentals=0),
                name="lay",
            )(place, cur.reshape(flat, tile_cols), x)
            up = lax.ppermute(low, GX, line(GX, 1))
            down_ = lax.ppermute(top, GX, line(GX, -1))
            from_left = lax.ppermute(right, "gy", line("gy", 1))
            from_right = lax.ppermute(left, "gy", line("gy", -1))
            got, y = lax.optimization_barrier((got, y))
        x = x + got
    own = x
    gathered = [own]
    for k in (1, 2, 3):
        gathered.append(lax.ppermute(own, "ens", ring("ens", -k)))
    own, one, two, three, up, down_, from_left, from_right = lax.optimization_barrier(
        (*gathered, up, down_, from_left, from_right)
    )
    stacked = jnp.stack([own, one, two, three])
    other = lax.ppermute(stacked, "gx_1", ring("gx_1", 1))
    pairs = batches * (batches - 1) // 2
    w, wc, wo = pl.pallas_call(
        taper_kernel,
        out_shape=[
            jax.ShapeDtypeStruct((batches * 10, n_obs, tile_cols), F32),
            jax.ShapeDtypeStruct((batches, n_obs, tile_cols), F32),
            jax.ShapeDtypeStruct((pairs, n_obs, n_obs), F32),
        ],
        in_specs=[smem, vmem, vmem, any_],
        out_specs=[vmem] * 3,
        compiler_params=pltpu.CompilerParams(vmem_limit_bytes=20 << 20),
        cost_estimate=pl.CostEstimate(flops=20_000_000, bytes_accessed=8_000_000, transcendentals=0),
        name="taper",
    )(place, obs_where, radius, stacked)
    out = pl.pallas_call(
        main_kernel,
        out_shape=jax.ShapeDtypeStruct((flat, tile_cols), F32),
        in_specs=[smem] + [vmem] * 16,
        out_specs=vmem,
        scratch_shapes=[
            VMEM((2, members, half), F32),
            VMEM((tile_rows + 2, members, here * tile_cols), F32),
            VMEM((members, tile_cols), F32),
            VMEM((n_obs, 3 * members), BF16),
            VMEM((2 * members, n_obs), BF16),
            VMEM((members, tile_cols), F32),
        ],
        compiler_params=pltpu.CompilerParams(vmem_limit_bytes=32 << 20),
        name="main",
    )(
        place, obs_value, obs_error, own, one, two, three, other,
        y, up, down_, from_left, from_right, w, wc, wo, wind,
    )
    out = out.reshape(levels, share_size, tile_rows, tile_cols)
    return lax.all_to_all(out, "ens", split_axis=0, concat_axis=0, tiled=True)


def solution(mesh):
    torus = Mesh(
        mesh.devices.reshape(8, 2, mesh.shape["gy"], mesh.shape["ens"]),
        ("gx_0", "gx_1", "gy", "ens"),
    )
    placed = (P(None, "ens", GX, "gy"), P(), P(), P(), P(), P(None, None, GX, "gy"))

    return jax.shard_map(
        shards, mesh=torus, in_specs=placed, out_specs=P(None, "ens", GX, "gy"), check_vma=False
    )
```

```python
import jax
import jax.numpy as jnp
from jax import lax
from jax.experimental import pallas as pl
from jax.experimental.pallas import tpu as pltpu
from jax.sharding import Mesh
from jax.sharding import PartitionSpec as P


GX = ("gx_0", "gx_1")
EPSILON = 1e-06
DIFFUSE = 0.05
F32 = jnp.float32
BF16 = jnp.bfloat16
ROWS = 5
VMEM = pltpu.VMEM
SMEM = pltpu.SMEM


def split(x):
    high = x.astype(BF16)
    return high, (x - high.astype(F32)).astype(BF16)


def pick_kernel(place_ref, where_ref, state_ref, keep_ref, give_ref, parts_ref, found_ref):
    row_start, col_start, core = place_ref[0], place_ref[1], place_ref[2]
    cells = state_ref.shape[0] // 8
    levels = found_ref.shape[0] // keep_ref.shape[0]
    members = keep_ref.shape[0]
    cols = state_ref.shape[1]
    n_obs = where_ref.shape[2]
    halves = where_ref.shape[0] // 2
    for row in range(8):
        x = state_ref[pl.ds(row, cells, stride=8), :]
        high = x.astype(BF16)
        rest = x - high.astype(F32)
        mid = rest.astype(BF16)
        low = (rest - mid.astype(F32)).astype(BF16)
        for at, part in enumerate((high, mid, low)):
            parts_ref[at * cells : (at + 1) * cells, row * cols : (row + 1) * cols] = part
    cell = lax.broadcasted_iota(jnp.int32, (8 * cols, n_obs), 0)
    for half, out_ref in enumerate((keep_ref, give_ref)):
        for at in range(halves):
            batch = lax.rem(core + half, 2) * halves + at
            places = where_ref[batch]
            lev = places[0:1, :]
            row = places[1:2, :] - row_start
            col = places[2:3, :] - col_start
            owned = (row >= 0) & (row < 8) & (col >= 0) & (col < cols)
            key = jnp.where(owned, row * cols + col, -1)
            hot = jnp.where(cell == key, 1.0, 0.0).astype(BF16)
            got = jnp.dot(parts_ref[...], hot, preferred_element_type=F32)
            found_ref[...] = got[:cells] + got[cells : 2 * cells] + got[2 * cells :]
            total = jnp.zeros((members, n_obs), F32)
            for level in range(levels):
                rows = found_ref[level * members : (level + 1) * members, :]
                total = total + jnp.where(lev == level, rows, 0.0)
            out_ref[:, at * n_obs : (at + 1) * n_obs] = total


def stack_kernel(own_ref, one_ref, two_ref, three_ref, inner_ref, out_ref):
    size = own_ref.shape[0]
    for at, ref in enumerate((own_ref, one_ref, two_ref, three_ref)):
        out_ref[at * size : (at + 1) * size, :] = ref[...]
    out_ref[4 * size :, :] = inner_ref[...]


def taper(dist_sq, reach):
    weight = jnp.maximum(0.0, 1.0 - dist_sq * reach)
    return weight * weight


def down(row):
    return jnp.transpose(jnp.broadcast_to(row, (128, row.shape[1])))


def wide(block, lanes):
    return jnp.concatenate([block] * (lanes // 128), axis=1)


def lay_kernel(place_ref, cur_ref, after_ref, y_ref, far_ref, near_ref, left_ref, right_ref):
    me = place_ref[3]
    cols = cur_ref.shape[1]
    shares = 4
    levels = y_ref.shape[2] // cols
    members = y_ref.shape[1] // shares
    for share in range(shares):
        source = lax.rem(me + share, shares)
        for level in range(levels):
            base = (source * levels + level) * members * 8
            for row in range(8):
                got = cur_ref[pl.ds(base + row, members, stride=8), :]
                y_ref[row, share * members : (share + 1) * members, level * cols : (level + 1) * cols] = got
    core = place_ref[2]
    far_ref[...] = y_ref[7 * core]
    near_ref[...] = y_ref[7 * (1 - core)]
    lane = lax.broadcasted_iota(jnp.int32, left_ref.shape, 1)
    left = jnp.zeros(left_ref.shape, F32)
    right = jnp.zeros(left_ref.shape, F32)
    for level in range(levels):
        for row in range(8):
            x = y_ref[row, :, level * cols : (level + 1) * cols]
            at = level * 8 + row
            left = jnp.where(lane == 32 + at, pltpu.roll(x, 32 + at, 1), left)
            right = jnp.where(lane == at, pltpu.roll(x, (at + 1) % cols, 1), right)
    left_ref[...] = left
    right_ref[...] = right


def taper_kernel(place_ref, where_ref, radius_ref, after_ref, w_ref, wc_ref, wo_ref):
    row_start, col_start = place_ref[0], place_ref[1]
    batches, _, n_obs = where_ref.shape
    cols = w_ref.shape[2]
    lane_w = lax.broadcasted_iota(jnp.int32, (n_obs, cols), 1)
    for batch in range(batches):
        places = where_ref[batch].astype(F32)
        q = radius_ref[batch : batch + 1, :].astype(F32)
        obs_row, obs_col = down(places[1:2, :]), down(places[2:3, :])
        reach = down(1.0 / (4.0 * q * q))
        gap = (lane_w + col_start).astype(F32) - obs_col
        gap = gap * gap
        for row in range(10):
            off = (row_start + (row - 1)).astype(F32) - obs_row
            w_ref[batch * 10 + row] = taper(off * off + gap, reach)
        edge_row = (row_start + lane_w % 8).astype(F32) - obs_row
        edge_col = jnp.where(lane_w < 32, col_start - 1, col_start + cols).astype(F32) - obs_col
        wc_ref[batch] = taper(edge_row * edge_row + edge_col * edge_col, reach)
        for later in range(batch + 1, batches):
            others = where_ref[later].astype(F32)
            off = others[1:2, :] - wide(obs_row, n_obs)
            gap_o = others[2:3, :] - wide(obs_col, n_obs)
            pair = batch * (2 * batches - batch - 1) // 2 + later - batch - 1
            wo_ref[pair] = taper(off * off + gap_o * gap_o, wide(reach, n_obs))


def changed(xs, weights, s3, n2):
    members = xs[0].shape[0]
    stacks = []
    for x in xs:
        mean = jnp.sum(x, axis=0, keepdims=True) * (1.0 / members)
        a_high, a_low = split(x - mean)
        stacks.append(jnp.concatenate([a_high, a_high, a_low], axis=0))
    covars = [jnp.dot(s3, a3, preferred_element_type=F32) for a3 in stacks]
    gains = [split(w * c) for w, c in zip(weights, covars)]
    outs = []
    for x, (g_high, g_low) in zip(xs, gains):
        both = jnp.dot(n2, g_high, preferred_element_type=F32)
        rest = jnp.dot(n2[:members], g_low, preferred_element_type=F32)
        outs.append(x + ((both[:members] + both[members:]) + rest))
    return outs


def posterior(z_ref, w_ref, batch, s3, n2):
    def step(at, carry):
        rows = [ROWS * at + k for k in range(ROWS)]
        xs = [z_ref[row] for row in rows]
        ws = [wide(w_ref[batch * 10 + row], z_ref.shape[2]) for row in rows]
        for row, out in zip(rows, changed(xs, ws, s3, n2)):
            z_ref[row] = out
        return carry

    lax.fori_loop(0, 10 // ROWS, step, 0)


def take_rows(span, place_ref, y_ref, far_ref, pack_ref, z_ref):
    core = place_ref[2]
    members = z_ref.shape[1]
    z_ref[9 * core] = far_ref[:, span]
    z_ref[9 * (1 - core)] = pack_ref[members:, span]
    for row in range(8):
        z_ref[row + 1] = y_ref[row, :, span]


def transported(first, place_ref, z_ref, edge_ref, wind_ref, f_ref, out_refs):
    lev_start = place_ref[4]
    members = z_ref.shape[1]
    cols = edge_ref.shape[1]
    levels = z_ref.shape[2] // cols
    share_size = members // len(out_refs)
    lane = lax.broadcasted_iota(jnp.int32, (members, cols), 1)

    def transport(row, carry):
        edge = edge_ref[...]
        for level in range(levels):
            span = slice(level * cols, (level + 1) * cols)
            a = wind_ref[0, lev_start + first + level, pl.ds(row, 1), :]
            b = wind_ref[1, lev_start + first + level, pl.ds(row, 1), :]
            to_up = jnp.maximum(a, 0.0) + DIFFUSE
            to_down = DIFFUSE - jnp.minimum(a, 0.0)
            to_left = jnp.maximum(b, 0.0) + DIFFUSE
            to_right = DIFFUSE - jnp.minimum(b, 0.0)
            stay = 1.0 - ((to_up + to_down) + (to_left + to_right))
            x = z_ref[row + 1, :, span]
            at = (first + level) * 8 + row
            left = jnp.where(lane == 0, pltpu.roll(edge, lax.rem(cols - at, cols), 1), pltpu.roll(x, 1, 1))
            right = jnp.where(
                lane == cols - 1, pltpu.roll(edge, cols - 33 - at, 1), pltpu.roll(x, cols - 1, 1)
            )
            f_ref[level] = (
                stay * x + to_up * z_ref[row, :, span] + to_down * z_ref[row + 2, :, span]
                + to_left * left + to_right * right
            )
            for share, out_ref in enumerate(out_refs):
                out_ref[pl.ds(level * share_size * 8 + row, share_size, stride=8), :] = f_ref[
                    level, share * share_size : (share + 1) * share_size, :
                ]
        return carry

    lax.fori_loop(0, 8, transport, 0)


def first_kernel(
    place_ref, value_ref, error_ref, own_ref, one_ref, two_ref, three_ref, pack_ref,
    y_ref, far_ref, left_ref, right_ref, w_ref, wc_ref, wo_ref, wind_ref,
    out0_ref, out1_ref, out2_ref, out3_ref, s3_ref, n2_ref, edge_ref, prior_ref, z_ref, f_ref,
):
    core = place_ref[2]
    batches, n_obs = value_ref.shape
    members = z_ref.shape[1]
    shares = 4
    share_size = members // shares
    half = own_ref.shape[1]
    for share, ref in enumerate((own_ref, one_ref, two_ref, three_ref)):
        rows = slice(share * share_size, (share + 1) * share_size)
        prior_ref[core, rows, :] = ref[...]
    prior_ref[1 - core] = pack_ref[:members]
    take_rows(slice(0, z_ref.shape[2]), place_ref, y_ref, far_ref, pack_ref, z_ref)
    edge_ref[...] = left_ref[...] + right_ref[...]
    per_half = half // n_obs

    def lanes(batch):
        at = batch % per_half
        return batch // per_half, slice(at * n_obs, (at + 1) * n_obs)

    for batch in range(batches):
        part, here = lanes(batch)
        priors = prior_ref[part, :, here]
        value, error = value_ref[batch : batch + 1, :], error_ref[batch : batch + 1, :]
        center = jnp.sum(priors, axis=0, keepdims=True) * (1.0 / members)
        spread = priors - center
        variance = jnp.sum(spread * spread, axis=0, keepdims=True) / (members - 1)
        summed = variance + error
        post_mean = (error * center + variance * value) / summed
        factor = jnp.sqrt(error / summed)
        nudges = post_mean + factor * spread - priors
        inverse = 1.0 / ((members - 1) * (variance + EPSILON))
        n_high, n_low = split(nudges * inverse)
        n2 = jnp.concatenate([n_high, n_low], axis=0)
        s_high, s_low = split(spread)
        s3 = jnp.concatenate([s_high.astype(F32), s_low.astype(F32), s_high.astype(F32)], axis=0)
        s3 = jnp.transpose(s3).astype(BF16)
        n2_ref[batch] = n2
        s3_ref[batch] = s3
        laters = range(batch + 1, batches)
        first = batch * (2 * batches - batch - 1) // 2
        blocks = [edge_ref[...]] + [prior_ref[lanes(k)[0], :, lanes(k)[1]] for k in laters]
        tapers = [wc_ref[batch]] + [wo_ref[first + k] for k in range(len(laters))]
        blocks = changed(blocks, tapers, s3, n2)
        edge_ref[...] = blocks[0]
        for k, block in zip(laters, blocks[1:]):
            prior_ref[lanes(k)[0], :, lanes(k)[1]] = block
        posterior(z_ref, w_ref, batch, s3_ref[batch], n2_ref[batch])
    transported(0, place_ref, z_ref, edge_ref, wind_ref, f_ref, (out0_ref, out1_ref, out2_ref, out3_ref))


def second_kernel(
    place_ref, pack_ref, y_ref, far_ref, s3_ref, n2_ref, edge_ref, w_ref, wind_ref,
    out0_ref, out1_ref, out2_ref, out3_ref, z_ref, f_ref,
):
    width = z_ref.shape[2]
    first = width // edge_ref.shape[1]
    take_rows(slice(width, 2 * width), place_ref, y_ref, far_ref, pack_ref, z_ref)
    for batch in range(s3_ref.shape[0]):
        posterior(z_ref, w_ref, batch, s3_ref[batch], n2_ref[batch])
    transported(first, place_ref, z_ref, edge_ref, wind_ref, f_ref, (out0_ref, out1_ref, out2_ref, out3_ref))


def place_kernel(place_ref, *refs):
    blocks, out_ref, sems = refs[:8], refs[8], refs[9]
    me = place_ref[3]
    length = blocks[0].shape[0]
    copies = []
    for at, block in enumerate(blocks):
        source = lax.rem(me + 4 - at % 4, 4)
        start = pl.multiple_of((source * 2 + at // 4) * length, length)
        copies.append(pltpu.make_async_copy(block, out_ref.at[pl.ds(start, length)], sems.at[at]))
    for copy in copies:
        copy.start()
    for copy in copies:
        copy.wait()


def ring(axis, shift):
    n = lax.axis_size(axis)
    return [(i, (i + shift) % n) for i in range(n)]


def line(axis, shift):
    n = lax.axis_size(axis)
    return [(i, i + shift) for i in range(n) if 0 <= i + shift < n]


def beyond():
    n = lax.axis_size(GX)
    return [(i, i - 1) for i in range(2, n, 2)] + [(i, i + 1) for i in range(1, n - 1, 2)]


def exchanges():
    cores = lax.axis_size("gx_1")
    depth, across = lax.axis_size("gx_0"), lax.axis_size("gy")
    far = [1 << k for k in range(depth.bit_length() - 1)]
    near = [1 << k for k in range(across.bit_length() - 1)]
    orders = (
        [("x", b) for b in near] + [("z", b) for b in far],
        [("z", b) for b in reversed(far)] + [("x", b) for b in near],
    )
    steps = []
    for at in range(len(orders[0])):
        pairs = []
        for z in range(depth):
            for core in range(cores):
                for x in range(across):
                    axis, bit = orders[core % 2][at]
                    to_z, to_x = (z ^ bit, x) if axis == "z" else (z, x ^ bit)
                    pairs.append(((z * cores + core) * across + x, (to_z * cores + core) * across + to_x))
        steps.append(pairs)
    return steps


def shards(state, obs_value, obs_error, obs_where, radius, wind):
    levels, share_size, tile_rows, tile_cols = state.shape
    shares = lax.axis_size("ens")
    members = share_size * shares
    here = levels // shares
    batches, n_obs = obs_value.shape
    half = batches // 2 * n_obs
    me = lax.axis_index("ens")
    place = jnp.stack(
        [lax.axis_index(GX) * tile_rows, lax.axis_index("gy") * tile_cols, lax.axis_index("gx_1"), me, me * here]
    ).astype(jnp.int32)
    flat = levels * share_size * tile_rows
    vmem = pl.BlockSpec(memory_space=VMEM)
    smem = pl.BlockSpec(memory_space=SMEM)
    cells = levels * share_size
    keep, give = pl.pallas_call(
        pick_kernel,
        out_shape=[jax.ShapeDtypeStruct((share_size, half), F32)] * 2,
        in_specs=[smem, vmem, vmem],
        out_specs=[vmem, vmem],
        scratch_shapes=[VMEM((3 * cells, tile_rows * tile_cols), BF16), VMEM((cells, n_obs), F32)],
        compiler_params=pltpu.CompilerParams(vmem_limit_bytes=16 << 20),
        name="pick",
    )(place, obs_where, state.reshape(flat, tile_cols))
    any_ = pl.BlockSpec(memory_space=pl.ANY)
    cur = lax.all_to_all(state, "ens", split_axis=0, concat_axis=0, tiled=True)
    x = keep + lax.ppermute(give, "gx_1", ring("gx_1", 1))
    for step, pairs in enumerate(exchanges(), start=1):
        got = lax.ppermute(x, (*GX, "gy"), pairs)
        if step == 3:
            line_shape = jax.ShapeDtypeStruct((members, here * tile_cols), F32)
            edge_shape = jax.ShapeDtypeStruct((members, tile_cols), F32)
            y, outer, inner, left, right = pl.pallas_call(
                lay_kernel,
                out_shape=[
                    jax.ShapeDtypeStruct((tile_rows, members, here * tile_cols), F32),
                    line_shape, line_shape, edge_shape, edge_shape,
                ],
                in_specs=[smem, vmem, any_],
                out_specs=[vmem] * 5,
                compiler_params=pltpu.CompilerParams(vmem_limit_bytes=12 << 20),
                cost_estimate=pl.CostEstimate(flops=2_000_000, bytes_accessed=4_000_000, transcendentals=0),
                name="lay",
            )(place, cur.reshape(flat, tile_cols), x)
            far = lax.ppermute(outer, GX, beyond())
            from_left = lax.ppermute(right, "gy", line("gy", 1))
            from_right = lax.ppermute(left, "gy", line("gy", -1))
            got, y = lax.optimization_barrier((got, y))
        x = x + got
    own = x
    gathered = [own]
    for k in (1, 2, 3):
        gathered.append(lax.ppermute(own, "ens", ring("ens", -k)))
    own, one, two, three, far, from_left, from_right = lax.optimization_barrier((*gathered, far, from_left, from_right))
    stacked = pl.pallas_call(
        stack_kernel,
        out_shape=jax.ShapeDtypeStruct((2 * members, half), F32),
        in_specs=[vmem] * 5,
        out_specs=vmem,
        compiler_params=pltpu.CompilerParams(vmem_limit_bytes=4 << 20),
        name="stack",
    )(own, one, two, three, inner)
    pack = lax.ppermute(stacked, "gx_1", ring("gx_1", 1))
    pairs = batches * (batches - 1) // 2
    w, wc, wo = pl.pallas_call(
        taper_kernel,
        out_shape=[
            jax.ShapeDtypeStruct((batches * 10, n_obs, tile_cols), F32),
            jax.ShapeDtypeStruct((batches, n_obs, tile_cols), F32),
            jax.ShapeDtypeStruct((pairs, n_obs, n_obs), F32),
        ],
        in_specs=[smem, vmem, vmem, any_],
        out_specs=[vmem] * 3,
        compiler_params=pltpu.CompilerParams(vmem_limit_bytes=20 << 20),
        cost_estimate=pl.CostEstimate(flops=20_000_000, bytes_accessed=8_000_000, transcendentals=0),
        name="taper",
    )(place, obs_where, radius, stacked)
    width = here // 2 * tile_cols
    piece = jax.ShapeDtypeStruct((flat // 8, tile_cols), F32)
    scratch = [VMEM((tile_rows + 2, members, width), F32), VMEM((here // 2, members, tile_cols), F32)]
    *early, s3, n2, edge = pl.pallas_call(
        first_kernel,
        out_shape=[
            piece, piece, piece, piece,
            jax.ShapeDtypeStruct((batches, n_obs, 3 * members), BF16),
            jax.ShapeDtypeStruct((batches, 2 * members, n_obs), BF16),
            edge_shape,
        ],
        in_specs=[smem] + [vmem] * 15,
        out_specs=[vmem] * 7,
        scratch_shapes=[VMEM((2, members, half), F32), *scratch],
        compiler_params=pltpu.CompilerParams(vmem_limit_bytes=24 << 20),
        cost_estimate=pl.CostEstimate(flops=3_000_000_000, bytes_accessed=8_000_000, transcendentals=0),
        name="first",
    )(
        place, obs_value, obs_error, own, one, two, three, pack,
        y, far, from_left, from_right, w, wc, wo, wind,
    )
    back = [early[0]]
    for k in (1, 2, 3):
        back.append(lax.ppermute(early[k], "ens", ring("ens", k)))
    late = pl.pallas_call(
        second_kernel,
        out_shape=[piece] * 4,
        in_specs=[smem] + [vmem] * 8,
        out_specs=[vmem] * 4,
        scratch_shapes=scratch,
        compiler_params=pltpu.CompilerParams(vmem_limit_bytes=24 << 20),
        cost_estimate=pl.CostEstimate(flops=3_000_000_000, bytes_accessed=8_000_000, transcendentals=0),
        name="second",
    )(place, pack, y, far, s3, n2, edge, w, wind)
    back.append(late[0])
    for k in (1, 2, 3):
        back.append(lax.ppermute(late[k], "ens", ring("ens", k)))
    out = pl.pallas_call(
        place_kernel,
        out_shape=jax.ShapeDtypeStruct((flat, tile_cols), F32),
        in_specs=[smem] + [vmem] * 8,
        out_specs=any_,
        scratch_shapes=[pltpu.SemaphoreType.DMA((8,))],
        compiler_params=pltpu.CompilerParams(vmem_limit_bytes=8 << 20),
        name="place",
    )(place, *back)
    return out.reshape(levels, share_size, tile_rows, tile_cols)


def solution(mesh):
    torus = Mesh(
        mesh.devices.reshape(8, 2, mesh.shape["gy"], mesh.shape["ens"]),
        ("gx_0", "gx_1", "gy", "ens"),
    )
    placed = (P(None, "ens", GX, "gy"), P(), P(), P(), P(), P(None, None, GX, "gy"))

    return jax.shard_map(shards, mesh=torus, in_specs=placed, out_specs=P(None, "ens", GX, "gy"), check_vma=False)
```

```python
import functools

import jax
import jax.numpy as jnp
from jax import lax
from jax.experimental import pallas as pl
from jax.experimental.pallas import tpu as pltpu
from jax.sharding import Mesh
from jax.sharding import PartitionSpec as P


GX = ("gx_0", "gx_1")
EPSILON = 1e-06
DIFFUSE = 0.05
F32 = jnp.float32
BF16 = jnp.bfloat16
ROWS = 5
VMEM = pltpu.VMEM
SMEM = pltpu.SMEM


def split(x):
    high = x.astype(BF16)
    return high, (x - high.astype(F32)).astype(BF16)


def pick_kernel(
    place_ref, where_ref, state_ref, keep_ref, give_ref, cut0_ref, cut1_ref, cut2_ref, cut3_ref, parts_ref, found_ref
):
    row_start, col_start, core = place_ref[0], place_ref[1], place_ref[2]
    cells = state_ref.shape[0] // 8
    levels = found_ref.shape[0] // keep_ref.shape[0]
    members = keep_ref.shape[0]
    cols = state_ref.shape[1]
    n_obs = where_ref.shape[2]
    halves = where_ref.shape[1] // 2
    for row in range(8):
        x = state_ref[pl.ds(row, cells, stride=8), :]
        for at, part in enumerate(split(x)):
            parts_ref[at * cells : (at + 1) * cells, row * cols : (row + 1) * cols] = part
    cell = lax.broadcasted_iota(jnp.int32, (8 * cols, n_obs), 0)
    for half, out_ref in enumerate((keep_ref, give_ref)):
        for at in range(halves):
            batch = lax.rem(core + half, 2) * halves + at
            lev, row, col = (where_ref[k, pl.ds(batch, 1), :] for k in range(3))
            row = row - row_start
            col = col - col_start
            owned = (row >= 0) & (row < 8) & (col >= 0) & (col < cols)
            key = jnp.where(owned, row * cols + col, -1)
            hot = jnp.where(cell == key, 1.0, 0.0).astype(BF16)
            got = jnp.dot(parts_ref[...], hot, preferred_element_type=F32)
            found_ref[...] = got[:cells] + got[cells:]
            total = jnp.zeros((members, n_obs), F32)
            for level in range(levels):
                rows = found_ref[level * members : (level + 1) * members, :]
                total = total + jnp.where(lev == level, rows, 0.0)
            out_ref[:, at * n_obs : (at + 1) * n_obs] = total
    length = cut0_ref.shape[0]
    for share, ref in enumerate((cut0_ref, cut1_ref, cut2_ref, cut3_ref)):
        target = lax.rem(place_ref[3] + share, 4)
        ref[...] = state_ref[pl.ds(pl.multiple_of(target * length, length), length), :]


def stack_kernel(own_ref, one_ref, two_ref, three_ref, inner_ref, out_ref):
    size = own_ref.shape[0]
    for at, ref in enumerate((own_ref, one_ref, two_ref, three_ref)):
        out_ref[at * size : (at + 1) * size, :] = ref[...]
    out_ref[4 * size :, :] = inner_ref[...]


def taper(dist_sq, reach):
    weight = jnp.maximum(0.0, 1.0 - dist_sq * reach)
    return weight * weight


def down(row):
    return jnp.transpose(jnp.broadcast_to(row, (128, row.shape[1])))


def wide(block, lanes):
    return jnp.concatenate([block] * (lanes // 128), axis=1)


def lay_kernel(place_ref, own_ref, one_ref, two_ref, three_ref, after_ref, y_ref, far_ref, near_ref, left_ref, right_ref):
    cols = own_ref.shape[1]
    shares = 4
    levels = y_ref.shape[2] // cols
    members = y_ref.shape[1] // shares
    for share, cur_ref in enumerate((own_ref, one_ref, two_ref, three_ref)):
        for level in range(levels):
            for row in range(8):
                got = cur_ref[pl.ds(level * members * 8 + row, members, stride=8), :]
                y_ref[row, share * members : (share + 1) * members, level * cols : (level + 1) * cols] = got
    core = place_ref[2]
    far_ref[...] = y_ref[7 * core]
    near_ref[...] = y_ref[7 * (1 - core)]
    lane = lax.broadcasted_iota(jnp.int32, left_ref.shape, 1)
    left = jnp.zeros(left_ref.shape, F32)
    right = jnp.zeros(left_ref.shape, F32)
    for level in range(levels):
        for row in range(8):
            x = y_ref[row, :, level * cols : (level + 1) * cols]
            at = level * 8 + row
            left = jnp.where(lane == 32 + at, pltpu.roll(x, 32 + at, 1), left)
            right = jnp.where(lane == at, pltpu.roll(x, (at + 1) % cols, 1), right)
    left_ref[...] = left
    right_ref[...] = right


def row_taper_kernel(place_ref, where_ref, radius_ref, after_ref, w_ref):
    row_start, col_start = place_ref[0], place_ref[1]
    _, batches, n_obs = where_ref.shape
    cols = w_ref.shape[2]
    lane_w = lax.broadcasted_iota(jnp.int32, (n_obs, cols), 1)
    for batch in range(batches):
        places = where_ref[:, batch, :].astype(F32)
        q = radius_ref[batch : batch + 1, :].astype(F32)
        obs_row, obs_col = down(places[1:2, :]), down(places[2:3, :])
        reach = down(1.0 / (4.0 * q * q))
        gap = (lane_w + col_start).astype(F32) - obs_col
        gap = gap * gap
        for row in range(10):
            off = (row_start + (row - 1)).astype(F32) - obs_row
            w_ref[batch * 10 + row] = taper(off * off + gap, reach)


def taper_kernel(place_ref, where_ref, radius_ref, after_ref, wc_ref, wo_ref):
    row_start, col_start = place_ref[0], place_ref[1]
    _, batches, n_obs = where_ref.shape
    cols = wc_ref.shape[2]
    lane_w = lax.broadcasted_iota(jnp.int32, (n_obs, cols), 1)
    for batch in range(batches):
        places = where_ref[:, batch, :].astype(F32)
        q = radius_ref[batch : batch + 1, :].astype(F32)
        obs_row, obs_col = down(places[1:2, :]), down(places[2:3, :])
        reach = down(1.0 / (4.0 * q * q))
        edge_row = (row_start + lane_w % 8).astype(F32) - obs_row
        edge_col = jnp.where(lane_w < 32, col_start - 1, col_start + cols).astype(F32) - obs_col
        wc_ref[batch] = taper(edge_row * edge_row + edge_col * edge_col, reach)
        for later in range(batch + 1, batches):
            others = where_ref[:, later, :].astype(F32)
            off = others[1:2, :] - wide(obs_row, n_obs)
            gap_o = others[2:3, :] - wide(obs_col, n_obs)
            pair = batch * (2 * batches - batch - 1) // 2 + later - batch - 1
            wo_ref[pair] = taper(off * off + gap_o * gap_o, wide(reach, n_obs))


def changed(xs, weights, s3, n2):
    members = xs[0].shape[0]
    stacks = []
    for x in xs:
        mean = jnp.sum(x, axis=0, keepdims=True) * (1.0 / members)
        a_high, a_low = split(x - mean)
        stacks.append(jnp.concatenate([a_high, a_high, a_low], axis=0))
    covars = [jnp.dot(s3, a3, preferred_element_type=F32) for a3 in stacks]
    gains = [split(w * c) for w, c in zip(weights, covars)]
    outs = []
    for x, (g_high, g_low) in zip(xs, gains):
        both = jnp.dot(n2, g_high, preferred_element_type=F32)
        rest = jnp.dot(n2[:members], g_low, preferred_element_type=F32)
        outs.append(x + ((both[:members] + both[members:]) + rest))
    return outs


def posterior(z_ref, w_ref, batch, s3, n2):
    def step(at, carry):
        rows = [ROWS * at + k for k in range(ROWS)]
        xs = [z_ref[row] for row in rows]
        ws = [wide(w_ref[batch * 10 + row], z_ref.shape[2]) for row in rows]
        for row, out in zip(rows, changed(xs, ws, s3, n2)):
            z_ref[row] = out
        return carry

    lax.fori_loop(0, 10 // ROWS, step, 0)


def take_rows(span, place_ref, y_ref, far_ref, pack_ref, z_ref):
    core = place_ref[2]
    members = z_ref.shape[1]
    z_ref[9 * core] = far_ref[:, span]
    z_ref[9 * (1 - core)] = pack_ref[members:, span]
    for row in range(8):
        z_ref[row + 1] = y_ref[row, :, span]


def transported(first, place_ref, z_ref, edge_ref, wind_ref, f_ref, out_refs):
    lev_start = place_ref[4]
    members = z_ref.shape[1]
    cols = edge_ref.shape[1]
    levels = z_ref.shape[2] // cols
    share_size = members // len(out_refs)
    lane = lax.broadcasted_iota(jnp.int32, (members, cols), 1)

    def transport(row, carry):
        edge = edge_ref[...]
        for level in range(levels):
            span = slice(level * cols, (level + 1) * cols)
            a = wind_ref[0, lev_start + first + level, pl.ds(row, 1), :]
            b = wind_ref[1, lev_start + first + level, pl.ds(row, 1), :]
            to_up = jnp.maximum(a, 0.0) + DIFFUSE
            to_down = DIFFUSE - jnp.minimum(a, 0.0)
            to_left = jnp.maximum(b, 0.0) + DIFFUSE
            to_right = DIFFUSE - jnp.minimum(b, 0.0)
            stay = 1.0 - ((to_up + to_down) + (to_left + to_right))
            x = z_ref[row + 1, :, span]
            at = (first + level) * 8 + row
            left = jnp.where(lane == 0, pltpu.roll(edge, lax.rem(cols - at, cols), 1), pltpu.roll(x, 1, 1))
            right = jnp.where(
                lane == cols - 1, pltpu.roll(edge, cols - 33 - at, 1), pltpu.roll(x, cols - 1, 1)
            )
            f_ref[level] = (
                stay * x + to_up * z_ref[row, :, span] + to_down * z_ref[row + 2, :, span]
                + to_left * left + to_right * right
            )
            for share, out_ref in enumerate(out_refs):
                out_ref[pl.ds(level * share_size * 8 + row, share_size, stride=8), :] = f_ref[
                    level, share * share_size : (share + 1) * share_size, :
                ]
        return carry

    lax.fori_loop(0, 8, transport, 0)


def first_kernel(
    place_ref, value_ref, error_ref, own_ref, one_ref, two_ref, three_ref, pack_ref,
    y_ref, far_ref, left_ref, right_ref, w_ref, wc_ref, wo_ref, wind_ref,
    out0_ref, out1_ref, out2_ref, out3_ref, s3_ref, n2_ref, edge_ref, prior_ref, z_ref, f_ref,
):
    core = place_ref[2]
    batches, n_obs = value_ref.shape
    members = z_ref.shape[1]
    shares = 4
    share_size = members // shares
    half = own_ref.shape[1]
    for share, ref in enumerate((own_ref, one_ref, two_ref, three_ref)):
        rows = slice(share * share_size, (share + 1) * share_size)
        prior_ref[core, rows, :] = ref[...]
    prior_ref[1 - core] = pack_ref[:members]
    take_rows(slice(0, z_ref.shape[2]), place_ref, y_ref, far_ref, pack_ref, z_ref)
    edge_ref[...] = left_ref[...] + right_ref[...]
    per_half = half // n_obs

    def lanes(batch):
        at = batch % per_half
        return batch // per_half, slice(at * n_obs, (at + 1) * n_obs)

    for batch in range(batches):
        part, here = lanes(batch)
        priors = prior_ref[part, :, here]
        value, error = value_ref[batch : batch + 1, :], error_ref[batch : batch + 1, :]
        center = jnp.sum(priors, axis=0, keepdims=True) * (1.0 / members)
        spread = priors - center
        variance = jnp.sum(spread * spread, axis=0, keepdims=True) / (members - 1)
        summed = variance + error
        post_mean = (error * center + variance * value) / summed
        factor = jnp.sqrt(error / summed)
        nudges = post_mean + factor * spread - priors
        inverse = 1.0 / ((members - 1) * (variance + EPSILON))
        n_high, n_low = split(nudges * inverse)
        n2 = jnp.concatenate([n_high, n_low], axis=0)
        s_high, s_low = split(spread)
        s3 = jnp.concatenate([s_high.astype(F32), s_low.astype(F32), s_high.astype(F32)], axis=0)
        s3 = jnp.transpose(s3).astype(BF16)
        n2_ref[batch] = n2
        s3_ref[batch] = s3
        laters = range(batch + 1, batches)
        first = batch * (2 * batches - batch - 1) // 2
        blocks = [edge_ref[...]] + [prior_ref[lanes(k)[0], :, lanes(k)[1]] for k in laters]
        tapers = [wc_ref[batch]] + [wo_ref[first + k] for k in range(len(laters))]
        blocks = changed(blocks, tapers, s3, n2)
        edge_ref[...] = blocks[0]
        for k, block in zip(laters, blocks[1:]):
            prior_ref[lanes(k)[0], :, lanes(k)[1]] = block
        posterior(z_ref, w_ref, batch, s3_ref[batch], n2_ref[batch])
    transported(0, place_ref, z_ref, edge_ref, wind_ref, f_ref, (out0_ref, out1_ref, out2_ref, out3_ref))


def second_kernel(
    place_ref, pack_ref, y_ref, far_ref, s3_ref, n2_ref, edge_ref, w_ref, wind_ref,
    out0_ref, out1_ref, out2_ref, out3_ref, z_ref, f_ref,
):
    width = z_ref.shape[2]
    first = width // edge_ref.shape[1]
    take_rows(slice(width, 2 * width), place_ref, y_ref, far_ref, pack_ref, z_ref)
    for batch in range(s3_ref.shape[0]):
        posterior(z_ref, w_ref, batch, s3_ref[batch], n2_ref[batch])
    transported(first, place_ref, z_ref, edge_ref, wind_ref, f_ref, (out0_ref, out1_ref, out2_ref, out3_ref))


def place_kernel(spots, place_ref, *refs):
    blocks, out_ref, sems = refs[: len(spots)], refs[-2], refs[-1]
    me = place_ref[3]
    length = blocks[0].shape[0]
    copies = []
    for at, ((back, half), block) in enumerate(zip(spots, blocks)):
        source = lax.rem(me + 4 - back, 4)
        start = pl.multiple_of((source * 2 + half) * length, length)
        copies.append(pltpu.make_async_copy(block, out_ref.at[pl.ds(start, length)], sems.at[at]))
    for copy in copies:
        copy.start()
    for copy in copies:
        copy.wait()


def ring(axis, shift):
    n = lax.axis_size(axis)
    return [(i, (i + shift) % n) for i in range(n)]


def line(axis, shift):
    n = lax.axis_size(axis)
    return [(i, i + shift) for i in range(n) if 0 <= i + shift < n]


def beyond():
    n = lax.axis_size(GX)
    return [(i, i - 1) for i in range(2, n, 2)] + [(i, i + 1) for i in range(1, n - 1, 2)]


def exchanges():
    cores = lax.axis_size("gx_1")
    depth, across = lax.axis_size("gx_0"), lax.axis_size("gy")
    far = [1 << k for k in range(depth.bit_length() - 1)]
    near = [1 << k for k in range(across.bit_length() - 1)]
    orders = (
        [("x", b) for b in near] + [("z", b) for b in far],
        [("z", b) for b in reversed(far)] + [("x", b) for b in near],
    )
    steps = []
    for at in range(len(orders[0])):
        pairs = []
        for z in range(depth):
            for core in range(cores):
                for x in range(across):
                    axis, bit = orders[core % 2][at]
                    to_z, to_x = (z ^ bit, x) if axis == "z" else (z, x ^ bit)
                    pairs.append(((z * cores + core) * across + x, (to_z * cores + core) * across + to_x))
        steps.append([pairs])
    return steps


def shards(state, obs_value, obs_error, obs_where, radius, wind):
    levels, share_size, tile_rows, tile_cols = state.shape
    shares = lax.axis_size("ens")
    members = share_size * shares
    here = levels // shares
    batches, n_obs = obs_value.shape
    half = batches // 2 * n_obs
    me = lax.axis_index("ens")
    place = jnp.stack(
        [lax.axis_index(GX) * tile_rows, lax.axis_index("gy") * tile_cols, lax.axis_index("gx_1"), me, me * here]
    ).astype(jnp.int32)
    flat = levels * share_size * tile_rows
    obs_where = jnp.swapaxes(obs_where, 0, 1)
    vmem = pl.BlockSpec(memory_space=VMEM)
    smem = pl.BlockSpec(memory_space=SMEM)
    cells = levels * share_size
    keep, give, *cuts = pl.pallas_call(
        pick_kernel,
        out_shape=[jax.ShapeDtypeStruct((share_size, half), F32)] * 2
        + [jax.ShapeDtypeStruct((flat // shares, tile_cols), F32)] * shares,
        in_specs=[smem, vmem, vmem],
        out_specs=[vmem] * 6,
        scratch_shapes=[VMEM((2 * cells, tile_rows * tile_cols), BF16), VMEM((cells, n_obs), F32)],
        compiler_params=pltpu.CompilerParams(vmem_limit_bytes=16 << 20),
        name="pick",
    )(place, obs_where, state.reshape(flat, tile_cols))
    any_ = pl.BlockSpec(memory_space=pl.ANY)
    x = keep + lax.ppermute(give, "gx_1", ring("gx_1", 1))
    for step, permutations in enumerate(exchanges(), start=1):
        got = [lax.ppermute(x, (*GX, "gy"), pairs) for pairs in permutations]
        if step == 1:
            came = []
            for k in (3, 2, 1):
                came.append(lax.ppermute(cuts[k], "ens", ring("ens", k)))
        if step == 4:
            line_shape = jax.ShapeDtypeStruct((members, here * tile_cols), F32)
            edge_shape = jax.ShapeDtypeStruct((members, tile_cols), F32)
            y, outer, inner, left, right = pl.pallas_call(
                lay_kernel,
                out_shape=[
                    jax.ShapeDtypeStruct((tile_rows, members, here * tile_cols), F32),
                    line_shape, line_shape, edge_shape, edge_shape,
                ],
                in_specs=[smem, vmem, vmem, vmem, vmem, any_],
                out_specs=[vmem] * 5,
                compiler_params=pltpu.CompilerParams(vmem_limit_bytes=12 << 20),
                cost_estimate=pl.CostEstimate(flops=2_000_000, bytes_accessed=4_000_000, transcendentals=0),
                name="lay",
            )(place, cuts[0], *came, x)
            far = lax.ppermute(outer, GX, beyond())
            from_left = lax.ppermute(right, "gy", line("gy", 1))
            from_right = lax.ppermute(left, "gy", line("gy", -1))
            *got, y = lax.optimization_barrier((*got, y))
        x = x + sum(got[1:], got[0])
    own = x
    gathered = [own]
    for k in (1, 2, 3):
        gathered.append(lax.ppermute(own, "ens", ring("ens", -k)))
    w = pl.pallas_call(
        row_taper_kernel,
        out_shape=jax.ShapeDtypeStruct((batches * 10, n_obs, tile_cols), F32),
        in_specs=[smem, vmem, vmem, any_],
        out_specs=vmem,
        compiler_params=pltpu.CompilerParams(vmem_limit_bytes=12 << 20),
        cost_estimate=pl.CostEstimate(flops=15_000_000, bytes_accessed=6_000_000, transcendentals=0),
        name="row_taper",
    )(place, obs_where, radius, own)
    own, one, two, three, far, from_left, from_right = lax.optimization_barrier((*gathered, far, from_left, from_right))
    stacked = pl.pallas_call(
        stack_kernel,
        out_shape=jax.ShapeDtypeStruct((2 * members, half), F32),
        in_specs=[vmem] * 5,
        out_specs=vmem,
        compiler_params=pltpu.CompilerParams(vmem_limit_bytes=4 << 20),
        name="stack",
    )(own, one, two, three, inner)
    pack = lax.ppermute(stacked, "gx_1", ring("gx_1", 1))
    pairs = batches * (batches - 1) // 2
    wc, wo = pl.pallas_call(
        taper_kernel,
        out_shape=[
            jax.ShapeDtypeStruct((batches, n_obs, tile_cols), F32),
            jax.ShapeDtypeStruct((pairs, n_obs, n_obs), F32),
        ],
        in_specs=[smem, vmem, vmem, any_],
        out_specs=[vmem] * 2,
        compiler_params=pltpu.CompilerParams(vmem_limit_bytes=8 << 20),
        cost_estimate=pl.CostEstimate(flops=5_000_000, bytes_accessed=2_000_000, transcendentals=0),
        name="taper",
    )(place, obs_where, radius, stacked)
    width = here // 2 * tile_cols
    piece = jax.ShapeDtypeStruct((flat // 8, tile_cols), F32)
    scratch = [VMEM((tile_rows + 2, members, width), F32), VMEM((here // 2, members, tile_cols), F32)]
    *early, s3, n2, edge = pl.pallas_call(
        first_kernel,
        out_shape=[
            piece, piece, piece, piece,
            jax.ShapeDtypeStruct((batches, n_obs, 3 * members), BF16),
            jax.ShapeDtypeStruct((batches, 2 * members, n_obs), BF16),
            edge_shape,
        ],
        in_specs=[smem] + [vmem] * 15,
        out_specs=[vmem] * 7,
        scratch_shapes=[VMEM((2, members, half), F32), *scratch],
        compiler_params=pltpu.CompilerParams(vmem_limit_bytes=24 << 20),
        cost_estimate=pl.CostEstimate(flops=3_000_000_000, bytes_accessed=8_000_000, transcendentals=0),
        name="first",
    )(
        place, obs_value, obs_error, own, one, two, three, pack,
        y, far, from_left, from_right, w, wc, wo, wind,
    )
    back = []
    for k in (1, 2, 3):
        back.append(lax.ppermute(early[k], "ens", ring("ens", k)))
    late = pl.pallas_call(
        second_kernel,
        out_shape=[piece] * 4,
        in_specs=[smem] + [vmem] * 8,
        out_specs=[vmem] * 4,
        scratch_shapes=scratch,
        compiler_params=pltpu.CompilerParams(vmem_limit_bytes=24 << 20),
        cost_estimate=pl.CostEstimate(flops=3_000_000_000, bytes_accessed=8_000_000, transcendentals=0),
        name="second",
    )(place, pack, y, far, s3, n2, edge, w, wind)
    last = []
    for k in (1, 2, 3):
        last.append(lax.ppermute(late[k], "ens", ring("ens", k)))

    def placed(blocks, spots, out):
        more = [] if out is None else [out]
        return pl.pallas_call(
            functools.partial(place_kernel, spots),
            out_shape=jax.ShapeDtypeStruct((flat, tile_cols), F32),
            in_specs=[smem] + [vmem] * len(blocks) + [any_] * len(more),
            out_specs=any_,
            scratch_shapes=[pltpu.SemaphoreType.DMA((len(blocks),))],
            input_output_aliases={1 + len(blocks): 0} if more else {},
            compiler_params=pltpu.CompilerParams(vmem_limit_bytes=4 << 20),
            name="place",
        )(place, *blocks, *more)

    out = placed([early[0], *back, late[0]], ((0, 0), (1, 0), (2, 0), (3, 0), (0, 1)), None)
    out = placed(last, ((1, 1), (2, 1), (3, 1)), out)
    return out.reshape(levels, share_size, tile_rows, tile_cols)


def solution(mesh):
    torus = Mesh(
        mesh.devices.reshape(8, 2, mesh.shape["gy"], mesh.shape["ens"]),
        ("gx_0", "gx_1", "gy", "ens"),
    )
    placed = (P(None, "ens", GX, "gy"), P(), P(), P(), P(), P(None, None, GX, "gy"))

    return jax.shard_map(shards, mesh=torus, in_specs=placed, out_specs=P(None, "ens", GX, "gy"), check_vma=False)
```
